128 devices in a mesh: row: 16 (over y, x_lo, core), col: 4 (over z), ka: 2 (over x_hi).
Axes of the slice: x: 4 (x_hi: 2, x_lo: 2; x = x_hi * 2 + x_lo), y: 4, z: 4, core: 2. Of those that a mesh axis runs over, the one named last changes fastest.
Arguments:
- iterate: float32 [7168, 8192], P('row', ('col', 'ka')), may hold values from -0.046875 to 0.046875
Outputs:
- update: float32 [7168, 8192], P('row', ('col', 'ka'))
The draws below stay inside these ranges and needn't reach their ends.
All inputs are finite; a program needn't handle non-finite values.
Results may differ from the reference program's by a relative error of at most 0.025.
Values may be sent and summed in bfloat16 or wider, within the bound.
A program may use at most 128 MiB of HBM per device.

```python
import math
import jax
import jax.numpy as jnp

M = 7168
N = 8192


def steps_of(own_key, shape, split, least, top_value):
    def one(axis_at, blocks):
        draws = jax.random.uniform(jax.random.fold_in(jax.random.fold_in(own_key, 6), axis_at), (blocks,), jnp.float32, least / len(split), top_value / len(split))
        return jnp.repeat(jnp.exp(draws), shape[axis_at] // blocks).reshape((-1,) + (1,) * (len(shape) - axis_at - 1))

    loudness = one(*split[0])
    for cut in split[1:]:
        loudness = loudness * one(*cut)
    return loudness


def scatter_about(own_key, extent, deviation, reach, split=(), kind=jnp.bfloat16):
    values = deviation * jax.random.normal(own_key, extent, jnp.float32)
    if split:
        values = values * steps_of(own_key, extent, split, -0.22, 0.18)
    return jnp.clip(values, -reach, reach).astype(kind)


def setup_inputs(seed: int = 0) -> dict:
    key_of = jax.random.split(jax.random.key(seed), 2)
    iterate = scatter_about(key_of[0], (M, N), (M + N) ** -0.5, 0.046875, ((0, 16), (1, 8)), jnp.float32)
    return {"iterate": iterate}


coef_a = 3.4445
coef_b = -4.775
coef_c = 2.0315

def reference(iterate):
    rounded = iterate.astype(jnp.bfloat16)
    gram_full = jnp.dot(rounded, rounded.T, preferred_element_type=jnp.float32)
    gram_high = gram_full.astype(jnp.bfloat16)
    gram_low = (gram_full - gram_high.astype(jnp.float32)).astype(jnp.bfloat16)
    first_sum = jnp.dot(gram_high, rounded, preferred_element_type=jnp.float32) + jnp.dot(gram_low, rounded, preferred_element_type=jnp.float32)
    first_product = first_sum.astype(jnp.bfloat16)
    second_product = jnp.dot(gram_high, first_product, preferred_element_type=jnp.float32) + jnp.dot(gram_low, first_product, preferred_element_type=jnp.float32)
    update_scale = 0.2 * math.sqrt(max(M, N))
    return update_scale * (coef_a * rounded.astype(jnp.float32) + coef_b * first_product.astype(jnp.float32) + coef_c * second_product)
```

```python
import math

import jax
import jax.numpy as jnp
from jax import lax
from jax.experimental import pallas as pl
from jax.experimental.pallas import tpu as pltpu
from jax.sharding import Mesh
from jax.sharding import PartitionSpec as P

M = 7168
N = 8192

coef_a = 3.4445
coef_b = -4.775
coef_c = 2.0315

BF = jnp.bfloat16
F32 = jnp.float32
MESH = pl.DeviceIdType.MESH

ROWS = 448
COLS = 1024
HALF = 224
Q = 112
BLK = 1792
SET = 896
NC = 4
CW = COLS // NC

B0, AP, AM, AC0, AC1, AC2, AC3, AFP, AFM = range(9)
BP, BM, BFP, BFM = range(9, 13)
GRS = 13
GAG = 19
FRS = 27
FAG = FRS + 3 * NC
SXC = FAG + 4 * NC
SRS = SXC + NC
NSEM = SRS + 3 * NC


def mod4(v):
    return lax.rem(v + 8, 4)


def kernel(x_ref, o_ref, A, B, GP, GR, G, FP, FR, F, SX, SC, SO, SP, SR, ss, rs):
    y = lax.axis_index("y")
    xl = lax.axis_index("xl")
    c = lax.axis_index("core")
    z = lax.axis_index("z")
    xh = lax.axis_index("xh")
    x = 2 * xh + xl

    def at(dx=0, dy=0, dz=0, dc=0):
        xx = mod4(x + dx)
        return (mod4(y + dy), lax.rem(xx, 2), lax.rem(c + dc, 2), mod4(z + dz), lax.div(xx, 2))

    peers = [at(dx=k) for k in (1, 2, 3)] + [at(dy=k) for k in (1, 2, 3)] + [at(dz=k) for k in (1, 2, 3)]
    peers.append(at(dc=1))
    barrier = pltpu.get_barrier_semaphore()
    for peer in peers:
        pl.semaphore_signal(barrier, inc=1, device_id=peer, device_id_type=MESH)

    def msg(src, dst, k, dev):
        return pltpu.make_async_remote_copy(
            src_ref=src, dst_ref=dst, send_sem=ss.at[k], recv_sem=rs.at[k], device_id=dev, device_id_type=MESH
        )

    def a_slot(dx, dc=0, off=0, size=ROWS):
        xx = mod4(x + dx)
        cc = lax.rem(c + dc, 2)
        row = pl.multiple_of((2 * cc + lax.rem(xx, 2)) * ROWS + off, 16)
        return A.at[lax.div(xx, 2), pl.ds(row, size)]

    def b_slot(dy):
        return B.at[mod4(y + dy)]

    own = a_slot(0)
    own[...] = x_ref[...].astype(BF)
    B[y, xh] = x_ref[pl.ds(pl.multiple_of(xh * HALF, 16), HALF), :].astype(BF)
    pl.semaphore_wait(barrier, len(peers))

    m_b0 = msg(a_slot(0, off=(1 - xh) * HALF, size=HALF), B.at[y, xh], B0, at(dx=2))
    m_ap = msg(own, own, AP, at(dx=1))
    m_am = msg(own, own, AM, at(dx=-1))
    m_ac = [msg(a_slot(d), a_slot(d), k, at(dc=1)) for d, k in ((0, AC0), (-1, AC1), (1, AC2), (2, AC3))]
    m_afp = msg(a_slot(-1, size=HALF), a_slot(-1, size=HALF), AFP, at(dx=1))
    m_afm = msg(a_slot(1, off=HALF, size=HALF), a_slot(1, off=HALF, size=HALF), AFM, at(dx=-1))
    m_bp = msg(b_slot(0), b_slot(0), BP, at(dy=1))
    m_bm = msg(b_slot(0), b_slot(0), BM, at(dy=-1))
    m_bfp = msg(b_slot(-1).at[0], b_slot(-1).at[0], BFP, at(dy=1))
    m_bfm = msg(b_slot(1).at[1], b_slot(1).at[1], BFM, at(dy=-1))

    m_b0.start()
    m_ap.start()
    m_am.start()
    m_ac[0].start()
    m_b0.wait_recv()
    m_bp.start()
    m_bm.start()
    m_ap.wait_recv()
    m_afp.start()
    m_ac[1].start()
    m_am.wait_recv()
    m_afm.start()
    m_ac[2].start()
    m_bp.wait_recv()
    m_bfp.start()
    m_bm.wait_recv()
    m_bfm.start()
    m_afp.wait_recv()
    m_afm.wait_recv()
    m_ac[3].start()
    for m in m_ac:
        m.wait_recv()

    def gram_piece(piece):
        def tile(t, carry):
            cols = pl.ds(pl.multiple_of(t * 256, 256), 256)
            acc = lax.dot_general(
                B[piece, 0], A[0, cols, :], (((1,), (1,)), ((), ())), preferred_element_type=F32
            ) + lax.dot_general(
                B[piece, 1], A[1, cols, :], (((1,), (1,)), ((), ())), preferred_element_type=F32
            )
            GP[piece, :, cols] = acc.astype(BF)
            return carry

        lax.fori_loop(0, BLK // 256, tile, 0)

    lax.fori_loop(0, 3, lambda k, s: (gram_piece(mod4(y - k - lax.div(k, 2))), s)[1], 0)
    m_bfp.wait_recv()
    m_bfm.wait_recv()
    gram_piece(mod4(y + 2))

    def g_cols(h):
        return pl.ds(h * SET, SET)

    def m_grs(h, k):
        return msg(GP.at[mod4(z + k), :, g_cols(h)], GR.at[k - 1, :, g_cols(h)], GRS + 3 * h + k - 1, at(dz=k))

    def g_rows(dz, off=0, size=HALF):
        return pl.ds(pl.multiple_of(mod4(z + dz) * HALF + off, 16), size)

    def m_gag(h, j):
        rows = (g_rows(0), g_rows(0), g_rows(-1, 0, Q), g_rows(1, Q, Q))[j]
        ref = G.at[rows, g_cols(h)]
        return msg(ref, ref, GAG + 4 * h + j, at(dz=(1, -1, 1, -1)[j]))

    for h in range(2):
        for k in (2, 1, 3):
            m_grs(h, k).start()
    for h in range(2):
        for k in (1, 2, 3):
            m_grs(h, k).wait_recv()
        total = GP[z, :, g_cols(h)].astype(F32)
        for k in range(3):
            total = total + GR[k, :, g_cols(h)].astype(F32)
        G[g_rows(0), g_cols(h)] = total.astype(BF)
        m_gag(h, 0).start()
        m_gag(h, 1).start()
    for h in range(2):
        m_gag(h, 0).wait_recv()
        m_gag(h, 2).start()
        m_gag(h, 1).wait_recv()
        m_gag(h, 3).start()
    for h in range(2):
        m_gag(h, 2).wait_recv()
        m_gag(h, 3).wait_recv()

    def m_frs(n, k):
        return msg(FP.at[n, mod4(y + k)], FR.at[n, k - 1], FRS + 3 * n + k - 1, at(dy=k))

    def f_rows(dy):
        return pl.ds(pl.multiple_of(mod4(y + dy) * HALF, 16), HALF)

    def m_fag(n, j):
        ref = (
            F.at[n, :, f_rows(0)],
            F.at[n, :, f_rows(0)],
            F.at[n, 0, f_rows(-1)],
            F.at[n, 1, f_rows(1)],
        )[j]
        return msg(ref, ref, FAG + 4 * n + j, at(dy=(1, -1, 1, -1)[j]))

    def m_sxc(n):
        return msg(SX.at[n], SC.at[n], SXC + n, at(dc=1))

    def m_srs(n, k):
        return msg(SP.at[n, mod4(x + k)], SR.at[n, k - 1], SRS + 3 * n + k - 1, at(dx=k))

    def chunk(n):
        return pl.ds(pl.multiple_of(n * CW, CW), CW)

    def first(n):
        for w in range(2):

            def piece(q, carry):
                rows = pl.ds(pl.multiple_of(q * HALF, 16), HALF)
                FP[n, q, w] = jnp.dot(G[rows, :], A[w, :, chunk(n)], preferred_element_type=F32).astype(BF)
                return carry

            lax.fori_loop(0, 4, piece, 0)
        for k in (2, 1, 3):
            m_frs(n, k).start()

    def first_sum(n):
        for k in (1, 2, 3):
            m_frs(n, k).wait_recv()
        for w in range(2):
            total = FP[n, y, w].astype(F32)
            for k in range(3):
                total = total + FR[n, k, w].astype(F32)
            F[n, w, f_rows(0), :] = total.astype(BF)
        m_fag(n, 0).start()
        m_fag(n, 1).start()

    def first_pass(n):
        m_fag(n, 0).wait_recv()
        m_fag(n, 2).start()
        m_fag(n, 1).wait_recv()
        m_fag(n, 3).start()

    def half_product(n, w, core, t):
        cols = pl.ds(pl.multiple_of(core * SET + t * 128, 128), 128)
        return lax.dot_general(G[:, cols], F[n, w], (((0,), (0,)), ((), ())), preferred_element_type=F32)

    def second(n):
        m_fag(n, 2).wait_recv()
        m_fag(n, 3).wait_recv()
        for w in range(2):

            def tile(t, carry):
                rows = pl.ds(pl.multiple_of(t * 128, 128), 128)
                SX[n, w, rows, :] = half_product(n, w, 1 - c, t).astype(BF)
                return carry

            lax.fori_loop(0, SET // 128, tile, 0)
        m_sxc(n).start()
        for w in range(2):

            def tile(t, carry):
                rows = pl.ds(pl.multiple_of(t * 128, 128), 128)
                SO[w, rows, :] = half_product(n, w, c, t)
                return carry

            lax.fori_loop(0, SET // 128, tile, 0)

    update_scale = 0.2 * math.sqrt(max(M, N))

    def second_sum(n):
        for w in range(2):
            rows = pl.ds(pl.multiple_of(xl * ROWS + xh * HALF, 16), HALF)
            SO[w, rows, :] = SO[w, rows, :] + (coef_b / coef_c) * F[n, w, f_rows(0), :].astype(F32)
        m_sxc(n).wait_recv()
        for xx in range(4):
            rows = pl.ds((xx % 2) * ROWS, ROWS)
            SP[n, xx] = (SO[xx // 2, rows, :] + SC[n, xx // 2, rows, :].astype(F32)).astype(BF)
        for k in (2, 1, 3):
            m_srs(n, k).start()

    def finish(n):
        for k in (1, 2, 3):
            m_srs(n, k).wait_recv()
        total = SP[n, x].astype(F32)
        for k in range(3):
            total = total + SR[n, k].astype(F32)
        rounded = x_ref[:, chunk(n)].astype(BF).astype(F32)
        o_ref[:, chunk(n)] = update_scale * (coef_a * rounded + coef_c * total)

    stages = ((0, first), (1, first_sum), (1, first_pass), (2, second), (2, second_sum), (3, finish))

    def step(t, carry):
        for lag, stage in stages:
            n = t - lag

            @pl.when((n >= 0) & (n < NC))
            def _():
                stage(n)

        return carry

    lax.fori_loop(0, NC + 3, step, 0)

    for m in [m_b0, m_ap, m_am, m_afp, m_afm, m_bp, m_bm, m_bfp, m_bfm] + m_ac:
        m.wait_send()
    for h in range(2):
        for k in (1, 2, 3):
            m_grs(h, k).wait_send()
        for j in range(4):
            m_gag(h, j).wait_send()

    def drain(n, carry):
        for k in (1, 2, 3):
            m_frs(n, k).wait_send()
            m_srs(n, k).wait_send()
        for j in range(4):
            m_fag(n, j).wait_send()
        m_sxc(n).wait_send()
        return carry

    lax.fori_loop(0, NC, drain, 0)


def body(iterate):
    vmem = pl.BlockSpec(memory_space=pltpu.VMEM)
    return pl.pallas_call(
        kernel,
        out_shape=jax.ShapeDtypeStruct((ROWS, COLS), F32),
        in_specs=[vmem],
        out_specs=vmem,
        scratch_shapes=[
            pltpu.VMEM((2, BLK, COLS), BF),
            pltpu.VMEM((4, 2, HALF, COLS), BF),
            pltpu.VMEM((4, HALF, BLK), BF),
            pltpu.VMEM((3, HALF, BLK), BF),
            pltpu.VMEM((SET, BLK), BF),
            pltpu.VMEM((NC, 4, 2, HALF, CW), BF),
            pltpu.VMEM((NC, 3, 2, HALF, CW), BF),
            pltpu.VMEM((NC, 2, SET, CW), BF),
            pltpu.VMEM((NC, 2, SET, CW), BF),
            pltpu.VMEM((NC, 2, SET, CW), BF),
            pltpu.VMEM((2, SET, CW), F32),
            pltpu.VMEM((NC, 4, ROWS, CW), BF),
            pltpu.VMEM((NC, 3, ROWS, CW), BF),
            pltpu.SemaphoreType.DMA((NSEM,)),
            pltpu.SemaphoreType.DMA((NSEM,)),
        ],
        compiler_params=pltpu.CompilerParams(
            collective_id=0, has_side_effects=True, vmem_limit_bytes=62 * 2**20
        ),
        cost_estimate=pl.CostEstimate(flops=20_000_000_000, bytes_accessed=4_000_000, transcendentals=0),
    )(iterate)


def solution(mesh):
    grid = Mesh(mesh.devices.reshape(4, 2, 2, 4, 2), ("y", "xl", "core", "z", "xh"))
    spec = P(("y", "xl", "core"), ("z", "xh"))
    return jax.shard_map(body, mesh=grid, in_specs=(spec,), out_specs=spec, check_vma=False)
```

```python
import math

import jax
import jax.numpy as jnp
from jax import lax
from jax.experimental import pallas as pl
from jax.experimental.pallas import tpu as pltpu
from jax.sharding import Mesh
from jax.sharding import PartitionSpec as P

M = 7168
N = 8192

coef_a = 3.4445
coef_b = -4.775
coef_c = 2.0315

BF = jnp.bfloat16
F32 = jnp.float32
MESH = pl.DeviceIdType.MESH

ROWS = 448
COLS = 1024
HALF = 224
Q = 112
BLK = 1792
SET = 896
NC = 4
CW = COLS // NC

SIZES = (64, 64, 96)
STARTS = (0, 64, 128)
LAGS = (0, 1, 2, 3, 5, 5, 6)


class Count:
    def __init__(self):
        self.n = 0

    def take(self):
        self.n += 1
        return self.n - 1


def mod4(v):
    return lax.rem(v + 8, 4)


def kernel(x_ref, o_ref, A, B, GP, GV, GR, G, GT, FP, FV, FR, F, SX, SC, SO, SP, SR, ss, rs):
    y = lax.axis_index("y")
    xl = lax.axis_index("xl")
    c = lax.axis_index("core")
    z = lax.axis_index("z")
    xh = lax.axis_index("xh")
    x = 2 * xh + xl
    count = Count()
    sent = []

    def at(dx=0, dy=0, dz=0, dc=0):
        xx = mod4(x + dx)
        return (mod4(y + dy), lax.rem(xx, 2), lax.rem(c + dc, 2), mod4(z + dz), lax.div(xx, 2))

    class Message:
        def __init__(self, src, dst, **to):
            k = count.take()
            self.copy = pltpu.make_async_remote_copy(
                src_ref=src, dst_ref=dst, send_sem=ss.at[k], recv_sem=rs.at[k], device_id=at(**to), device_id_type=MESH
            )
            sent.append(self.copy)
            self.copy.start()

        def wait(self):
            self.copy.wait_recv()

    def rows(start, size):
        return pl.ds(pl.multiple_of(start, 16), size)

    peers = [at(dx=k) for k in (1, 2, 3)] + [at(dy=k) for k in (1, 2, 3)] + [at(dz=k) for k in (1, 2, 3)]
    peers.append(at(dc=1))
    barrier = pltpu.get_barrier_semaphore()
    for peer in peers:
        pl.semaphore_signal(barrier, inc=1, device_id=peer, device_id_type=MESH)

    def a_slot(dx, off=0, size=ROWS):
        xx = mod4(x + dx)
        return A.at[lax.div(xx, 2), rows((2 * c + lax.rem(xx, 2)) * ROWS + off, size)]

    def near(dx):
        return lax.div(mod4(x + dx), 2) * HALF

    own = a_slot(0)
    own[...] = x_ref[...].astype(BF)
    B[y, xh] = x_ref[rows(near(0), HALF), :].astype(BF)
    pl.semaphore_wait(barrier, len(peers))

    def copy_slot(slot, off, size, **to):
        return Message(a_slot(slot, off, size), a_slot(slot, off, size), **to)

    far = near(2)
    m_far = copy_slot(0, far, HALF, dx=2)
    m_b1 = Message(B.at[y, xh], B.at[y, xh], dy=1)
    m_b2 = Message(B.at[y, xh], B.at[y, xh], dy=-1)
    m_a1 = copy_slot(0, 0, ROWS, dx=1)
    m_a2 = copy_slot(0, 0, ROWS, dx=-1)
    cores = [copy_slot(0, 0, ROWS, dc=1)]
    m_far.wait()
    half = a_slot(2, near(0), HALF)
    m_b3 = Message(half, B.at[y, 1 - xh], dy=1)
    m_b4 = Message(half, B.at[y, 1 - xh], dy=-1)
    cores.append(copy_slot(2, near(0), HALF, dc=1))
    B[y, 1 - xh] = half[...]
    m_b1.wait()
    m_b5 = Message(B.at[mod4(y - 1), xh], B.at[mod4(y - 1), xh], dy=1)
    m_a1.wait()
    m_a3 = copy_slot(-1, near(-1), Q, dx=1)
    cores.append(copy_slot(-1, 0, ROWS, dc=1))
    m_a2.wait()
    m_a4 = copy_slot(1, near(1) + Q, Q, dx=-1)
    cores.append(copy_slot(1, 0, ROWS, dc=1))
    m_b3.wait()
    m_b2.wait()
    m_b4.wait()
    m_b6 = Message(B.at[mod4(y + 1), 1 - xh], B.at[mod4(y + 1), 1 - xh], dy=-1)
    m_a3.wait()
    m_a4.wait()
    cores.append(copy_slot(2, near(2), HALF, dc=1))
    m_b5.wait()
    m_b6.wait()
    for m in cores:
        m.wait()

    def piece(r, q, off=0, size=None):
        return rows(4 * STARTS[r] + mod4(q) * SIZES[r] + off, SIZES[r] if size is None else size)

    def gram(r):
        part = slice(STARTS[r], STARTS[r] + SIZES[r])

        def tile(t, carry):
            cols = pl.ds(pl.multiple_of(t * 256, 256), 256)
            acc = jnp.zeros((4 * SIZES[r], 256), F32)
            for w in range(2):
                left = B[:, w, part, :].reshape(4 * SIZES[r], COLS)
                acc = acc + lax.dot_general(
                    left, A[w, cols, :], (((1,), (1,)), ((), ())), preferred_element_type=F32
                )
            GP[pl.ds(4 * STARTS[r], 4 * SIZES[r]), cols] = acc.astype(BF)
            return carry

        lax.fori_loop(0, BLK // 256, tile, 0)

    msgs = {}

    def z_far(r):
        h = SIZES[r] // 2
        msgs["zv", r] = [
            Message(GP.at[piece(r, z + 2, w * h, h)], GV.at[w, pl.ds(STARTS[r] // 2, h)], dz=1 - 2 * w) for w in range(2)
        ]

    def z_near(r):
        h = SIZES[r] // 2
        msgs["zr", r] = []
        for w, m in enumerate(msgs["zv", r]):
            m.wait()
            q = piece(r, z + 1 - 2 * w, w * h, h)
            GP[q, :] = (GP[q, :].astype(F32) + GV[w, pl.ds(STARTS[r] // 2, h), :].astype(F32)).astype(BF)
            msgs["zr", r].append(
                Message(GP.at[piece(r, z + 1 - 2 * w)], GR.at[w, pl.ds(STARTS[r], SIZES[r])], dz=1 - 2 * w)
            )

    def z_sum(r):
        for m in msgs["zr", r]:
            m.wait()
        part = pl.ds(STARTS[r], SIZES[r])
        total = GP[piece(r, z), :].astype(F32) + GR[0, part, :].astype(F32) + GR[1, part, :].astype(F32)
        G[piece(r, z), :] = total.astype(BF)
        ref = G.at[piece(r, z)]
        msgs["zg", r] = [Message(ref, ref, dz=1 - 2 * w) for w in range(2)]

    def z_pass(r):
        h = SIZES[r] // 2
        msgs["zp", r] = []
        for w, m in enumerate(msgs["zg", r]):
            m.wait()
            ref = G.at[piece(r, z - 1 + 2 * w, w * h, h)]
            msgs["zp", r].append(Message(ref, ref, dz=1 - 2 * w))

    def z_done(r):
        for m in msgs["zp", r]:
            m.wait()
        cols = slice(4 * STARTS[r], 4 * (STARTS[r] + SIZES[r]))
        for t in range(BLK // 256):
            GT[t * 256 : (t + 1) * 256, cols] = G[cols, t * 256 : (t + 1) * 256].T

    def f_first(r, n):
        for w in range(2):
            FP[n, w, pl.ds(4 * STARTS[r], 4 * SIZES[r]), :] = jnp.dot(
                G[pl.ds(4 * STARTS[r], 4 * SIZES[r]), :],
                A[w, :, n * CW : (n + 1) * CW],
                preferred_element_type=F32,
            ).astype(BF)
        part = pl.ds(STARTS[r], SIZES[r])
        msgs["fv", r, n] = [
            Message(FP.at[n, w, piece(r, y + 2)], FV.at[n, w, part], dy=1 - 2 * w) for w in range(2)
        ]

    def f_near(r, n):
        part = pl.ds(STARTS[r], SIZES[r])
        msgs["fr", r, n] = []
        for w, m in enumerate(msgs["fv", r, n]):
            m.wait()
            q = piece(r, y + 1 - 2 * w)
            FP[n, w, q, :] = (FP[n, w, q, :].astype(F32) + FV[n, w, part, :].astype(F32)).astype(BF)
            msgs["fr", r, n].append(Message(FP.at[n, :, q], FR.at[n, w, :, part], dy=1 - 2 * w))

    def f_sum(r, n):
        part = pl.ds(STARTS[r], SIZES[r])
        for m in msgs["fr", r, n]:
            m.wait()
        q = piece(r, y)
        for w in range(2):
            total = FP[n, w, q, :].astype(F32) + FR[n, 0, w, part, :].astype(F32) + FR[n, 1, w, part, :].astype(F32)
            F[n, w, q, :] = total.astype(BF)
        msgs["fg", r, n] = [Message(F.at[n, :, q], F.at[n, :, q], dy=1 - 2 * w) for w in range(2)]

    def f_pass(r, n):
        msgs["fp", r, n] = []
        for w, m in enumerate(msgs["fg", r, n]):
            m.wait()
            ref = F.at[n, w, piece(r, y - 1 + 2 * w)]
            msgs["fp", r, n].append(Message(ref, ref, dy=1 - 2 * w))

    def s_half(n, w, core):
        return jnp.dot(GT[rows(core * SET, SET), :], F[n, w], preferred_element_type=F32)

    def second(r, n):
        for m in msgs["fp", r, n]:
            m.wait()
        if r < len(SIZES) - 1:
            return
        for w in range(2):
            SX[n, w] = s_half(n, w, 1 - c).astype(BF)
        msgs["sx", n] = Message(SX.at[n], SC.at[n], dc=1)
        for w in range(2):
            SO[n % 2, w] = s_half(n, w, c)

    update_scale = 0.2 * math.sqrt(max(M, N))

    def second_sum(r, n):
        if r < len(SIZES) - 1:
            return
        for w in range(2):
            for k in range(len(SIZES)):
                q = rows(xl * ROWS + xh * HALF + STARTS[k], SIZES[k])
                SO[n % 2, w, q, :] = SO[n % 2, w, q, :] + (coef_b / coef_c) * F[n, w, piece(k, y), :].astype(F32)
        msgs["sx", n].wait()
        for xx in range(4):
            q = pl.ds((xx % 2) * ROWS, ROWS)
            SP[n, xx] = (SO[n % 2, xx // 2, q, :] + SC[n, xx // 2, q, :].astype(F32)).astype(BF)
        msgs["sr", n] = [Message(SP.at[n, mod4(x + k)], SR.at[n, k - 1], dx=k) for k in (2, 1, 3)]

    def finish(r, n):
        if r < len(SIZES) - 1:
            return
        for m in msgs["sr", n]:
            m.wait()
        cols = slice(n * CW, (n + 1) * CW)
        total = SP[n, x].astype(F32)
        for k in range(3):
            total = total + SR[n, k].astype(F32)
        rounded = x_ref[:, cols].astype(BF).astype(F32)
        o_ref[:, cols] = update_scale * (coef_a * rounded + coef_c * total)

    gram(0)
    z_far(0)
    gram(1)
    z_near(0)
    gram(2)
    z_far(1)
    z_sum(0)
    z_near(1)
    z_pass(0)
    z_done(0)

    steps = [(r, n) for r in range(len(SIZES)) for n in range(NC)]
    beside = {1: [(z_sum, 1), (z_far, 2)], 2: [(z_pass, 1), (z_near, 2)], 3: [(z_done, 1)]}
    beside.update({5: [(z_sum, 2)], 6: [(z_pass, 2)], 7: [(z_done, 2)]})
    stages = (f_first, f_near, f_sum, f_pass, second, second_sum, finish)
    for t in range(len(steps) + LAGS[-1]):
        for stage, lag in zip(stages, LAGS):
            if 0 <= t - lag < len(steps):
                stage(*steps[t - lag])
        for stage, r in beside.get(t, ()):
            stage(r)

    for copy in sent:
        copy.wait_send()


def body(iterate):
    vmem = pl.BlockSpec(memory_space=pltpu.VMEM)
    return pl.pallas_call(
        kernel,
        out_shape=jax.ShapeDtypeStruct((ROWS, COLS), F32),
        in_specs=[vmem],
        out_specs=vmem,
        scratch_shapes=[
            pltpu.VMEM((2, BLK, COLS), BF),
            pltpu.VMEM((4, 2, HALF, COLS), BF),
            pltpu.VMEM((SET, BLK), BF),
            pltpu.VMEM((2, Q, BLK), BF),
            pltpu.VMEM((2, HALF, BLK), BF),
            pltpu.VMEM((SET, BLK), BF),
            pltpu.VMEM((BLK, SET), BF),
            pltpu.VMEM((NC, 2, SET, CW), BF),
            pltpu.VMEM((NC, 2, HALF, CW), BF),
            pltpu.VMEM((NC, 2, 2, HALF, CW), BF),
            pltpu.VMEM((NC, 2, SET, CW), BF),
            pltpu.VMEM((NC, 2, SET, CW), BF),
            pltpu.VMEM((NC, 2, SET, CW), BF),
            pltpu.VMEM((2, 2, SET, CW), F32),
            pltpu.VMEM((NC, 4, ROWS, CW), BF),
            pltpu.VMEM((NC, 3, ROWS, CW), BF),
            pltpu.SemaphoreType.DMA((256,)),
            pltpu.SemaphoreType.DMA((256,)),
        ],
        compiler_params=pltpu.CompilerParams(
            collective_id=0, has_side_effects=True, vmem_limit_bytes=62 * 2**20
        ),
        cost_estimate=pl.CostEstimate(flops=20_000_000_000, bytes_accessed=4_000_000, transcendentals=0),
    )(iterate)


def solution(mesh):
    grid = Mesh(mesh.devices.reshape(4, 2, 2, 4, 2), ("y", "xl", "core", "z", "xh"))
    spec = P(("y", "xl", "core"), ("z", "xh"))
    return jax.shard_map(body, mesh=grid, in_specs=(spec,), out_specs=spec, check_vma=False)
```

```python
import math

import jax
import jax.numpy as jnp
from jax import lax
from jax.experimental import pallas as pl
from jax.experimental.pallas import tpu as pltpu
from jax.sharding import Mesh
from jax.sharding import PartitionSpec as P

M = 7168
N = 8192

coef_a = 3.4445
coef_b = -4.775
coef_c = 2.0315

BF = jnp.bfloat16
F32 = jnp.float32
MESH = pl.DeviceIdType.MESH

ROWS = 448
COLS = 1024
HALF = 224
Q = 112
BLK = 1792
SET = 896
WIDTHS = (256, 256, 256, 256)
NC = len(WIDTHS)
LEFT = tuple(sum(WIDTHS[:n]) for n in range(NC))

SIZES = (64, 64, 96)
STARTS = (0, 64, 128)
LAGS = (0, 1, 2, 3, 4, 4, 5, 6)


class Count:
    def __init__(self):
        self.n = 0

    def take(self):
        self.n += 1
        return self.n - 1


def mod4(v):
    return lax.rem(v + 8, 4)


def kernel(x_hbm, o_hbm, x_ref, o_ref, A, B, GP, GV, GR, G, GT, SO, *refs):
    FP, FV, FR, F, SX, SC, SP, SV, SR = [refs[k * NC : (k + 1) * NC] for k in range(9)]
    io, ss, rs = refs[9 * NC :]
    y = lax.axis_index("y")
    xl = lax.axis_index("xl")
    c = lax.axis_index("core")
    z = lax.axis_index("z")
    xh = lax.axis_index("xh")
    x = 2 * xh + xl
    count = Count()
    sent = []

    def at(dx=0, dy=0, dz=0, dc=0):
        xx = mod4(x + dx)
        return (mod4(y + dy), lax.rem(xx, 2), lax.rem(c + dc, 2), mod4(z + dz), lax.div(xx, 2))

    class Message:
        def __init__(self, src, dst, **to):
            k = count.take()
            self.copy = pltpu.make_async_remote_copy(
                src_ref=src, dst_ref=dst, send_sem=ss.at[k], recv_sem=rs.at[k], device_id=at(**to), device_id_type=MESH
            )
            sent.append(self.copy)
            self.copy.start()

        def wait(self):
            self.copy.wait_recv()

    def rows(start, size):
        return pl.ds(pl.multiple_of(start, 16), size)

    peers = [at(dx=k) for k in (1, 2, 3)] + [at(dy=k) for k in (1, 2, 3)] + [at(dz=k) for k in (1, 2, 3)]
    peers.append(at(dc=1))
    barrier = pltpu.get_barrier_semaphore()
    for peer in peers:
        pl.semaphore_signal(barrier, inc=1, device_id=peer, device_id_type=MESH)

    def a_slot(dx, off=0, size=ROWS):
        xx = mod4(x + dx)
        return A.at[lax.div(xx, 2), rows((2 * lax.rem(xx, 2) + c) * ROWS + off, size)]

    def near(dx):
        return lax.div(mod4(x + dx), 2) * HALF

    load = pltpu.make_async_copy(x_hbm, x_ref, io.at[0])
    load.start()
    load.wait()
    own = a_slot(0)
    own[...] = x_ref[...].astype(BF)
    B[y, xh] = x_ref[rows(near(0), HALF), :].astype(BF)
    pl.semaphore_wait(barrier, len(peers))

    def copy_slot(slot, off, size, **to):
        return Message(a_slot(slot, off, size), a_slot(slot, off, size), **to)

    def copy_b(step, w, off, size, **to):
        ref = B.at[mod4(y + step), w, pl.ds(off, size)]
        return Message(ref, ref, **to)

    def both(make):
        return [make(1 - 2 * w, w) for w in range(2)]

    m_far = copy_slot(0, near(2), HALF, dx=2)
    m_b = both(lambda d, w: copy_b(0, xh, 0, HALF, dy=d))
    m_a = both(lambda d, w: copy_slot(0, near(0), HALF, dx=d))
    m_a += both(lambda d, w: copy_slot(0, near(2), HALF, dx=d))
    cores = [copy_slot(0, 0, ROWS, dc=1)]
    m_bp = []
    for w, m in enumerate(m_b):
        m.wait()
        m_bp.append(copy_b(2 * w - 1, xh, w * Q, Q, dy=1 - 2 * w))
    m_far.wait()
    half = a_slot(2, near(0), HALF)
    m_c = both(lambda d, w: Message(half, B.at[y, 1 - xh], dy=d))
    cores.append(copy_slot(2, near(0), HALF, dc=1))
    B[y, 1 - xh] = half[...]
    m_ap = []
    for w in range(2):
        m_a[w].wait()
        m_ap.append(copy_slot(2 * w - 1, near(2 * w - 1) + w * Q, Q, dx=1 - 2 * w))
    for w, m in enumerate(m_c):
        m.wait()
        m_bp.append(copy_b(2 * w - 1, 1 - xh, w * Q, Q, dy=1 - 2 * w))
    for w in range(2):
        m_a[2 + w].wait()
        cores.append(copy_slot(2 * w - 1, 0, ROWS, dc=1))
    for m in m_bp + cores:
        m.wait()

    def gather_end():
        for m in m_ap:
            m.wait()
        copy_slot(2, near(2), HALF, dc=1).wait()

    def piece(r, q, off=0, size=None):
        return rows(4 * STARTS[r] + mod4(q) * SIZES[r] + off, SIZES[r] if size is None else size)

    def cols_of(k):
        return pl.ds(pl.multiple_of((1 - xl if k == 0 else xl) * SET, 128), SET)

    def gram(r, k):
        cols = cols_of(k)
        acc = jnp.zeros((4 * SIZES[r], SET), F32)
        for w in range(2):
            left = B[:, w, STARTS[r] : STARTS[r] + SIZES[r], :].reshape(4 * SIZES[r], COLS)
            acc = acc + lax.dot_general(left, A[w, cols, :], (((1,), (1,)), ((), ())), preferred_element_type=F32)
        GP[pl.ds(4 * STARTS[r], 4 * SIZES[r]), cols] = acc.astype(BF)

    msgs = {}

    def z_far(r, k):
        h = SIZES[r] // 2
        msgs["zv", r, k] = both(
            lambda d, w: Message(
                GP.at[piece(r, z + 2, w * h, h), cols_of(k)], GV.at[w, pl.ds(STARTS[r] // 2, h), cols_of(k)], dz=d
            )
        )

    def z_near(r, k):
        h = SIZES[r] // 2
        msgs["zr", r, k] = []
        for w, m in enumerate(msgs["zv", r, k]):
            m.wait()
            q, cols = piece(r, z + 1 - 2 * w, w * h, h), cols_of(k)
            GP[q, cols] = (GP[q, cols].astype(F32) + GV[w, pl.ds(STARTS[r] // 2, h), cols].astype(F32)).astype(BF)
            msgs["zr", r, k].append(
                Message(
                    GP.at[piece(r, z + 1 - 2 * w), cols], GR.at[w, pl.ds(STARTS[r], SIZES[r]), cols], dz=1 - 2 * w
                )
            )

    def z_sum(r, k):
        for m in msgs["zr", r, k]:
            m.wait()
        part, cols = pl.ds(STARTS[r], SIZES[r]), cols_of(k)
        total = GP[piece(r, z), cols].astype(F32) + GR[0, part, cols].astype(F32) + GR[1, part, cols].astype(F32)
        G[piece(r, z), cols] = total.astype(BF)
        ref = G.at[piece(r, z), cols]
        msgs["zg", r, k] = both(lambda d, w: Message(ref, ref, dz=d))

    def z_pass(r, k):
        h = SIZES[r] // 2
        msgs["zp", r, k] = []
        for w, m in enumerate(msgs["zg", r, k]):
            m.wait()
            ref = G.at[piece(r, z - 1 + 2 * w, w * h, h), cols_of(k)]
            msgs["zp", r, k].append(Message(ref, ref, dz=1 - 2 * w))

    def z_done(r):
        for m in msgs["zp", r, 0] + msgs["zp", r, 1]:
            m.wait()

    def transpose(r):
        cols = slice(4 * STARTS[r], 4 * (STARTS[r] + SIZES[r]))
        for t in range(BLK // 256):
            GT[t * 256 : (t + 1) * 256, cols] = G[cols, t * 256 : (t + 1) * 256].T

    def f_first(r, n):
        for w in range(2):
            FP[n][w, pl.ds(4 * STARTS[r], 4 * SIZES[r]), :] = jnp.dot(
                G[pl.ds(4 * STARTS[r], 4 * SIZES[r]), :],
                A[w, :, LEFT[n] : LEFT[n] + WIDTHS[n]],
                preferred_element_type=F32,
            ).astype(BF)
        part = pl.ds(STARTS[r], SIZES[r])
        msgs["fv", r, n] = [
            Message(FP[n].at[w, piece(r, y + 2)], FV[n].at[w, part], dy=1 - 2 * w) for w in range(2)
        ]

    def f_near(r, n):
        part = pl.ds(STARTS[r], SIZES[r])
        msgs["fr", r, n] = []
        for w, m in enumerate(msgs["fv", r, n]):
            m.wait()
            q = piece(r, y + 1 - 2 * w)
            FP[n][w, q, :] = (FP[n][w, q, :].astype(F32) + FV[n][w, part, :].astype(F32)).astype(BF)
            msgs["fr", r, n].append(Message(FP[n].at[:, q], FR[n].at[w, :, part], dy=1 - 2 * w))

    def f_sum(r, n):
        part = pl.ds(STARTS[r], SIZES[r])
        for m in msgs["fr", r, n]:
            m.wait()
        q = piece(r, y)
        for w in range(2):
            total = FP[n][w, q, :].astype(F32) + FR[n][0, w, part, :].astype(F32) + FR[n][1, w, part, :].astype(F32)
            F[n][w, q, :] = total.astype(BF)
        msgs["fg", r, n] = [Message(F[n].at[:, q], F[n].at[:, q], dy=1 - 2 * w) for w in range(2)]

    def f_pass(r, n):
        msgs["fp", r, n] = []
        for w, m in enumerate(msgs["fg", r, n]):
            m.wait()
            ref = F[n].at[w, piece(r, y - 1 + 2 * w)]
            msgs["fp", r, n].append(Message(ref, ref, dy=1 - 2 * w))

    def s_half(n, w, core):
        left = [GT[rows(k * SET + core * ROWS, ROWS), :] for k in range(2)]
        return jnp.dot(jnp.concatenate(left, axis=0), F[n][w], preferred_element_type=F32)

    def second(r, n):
        for m in msgs["fp", r, n]:
            m.wait()
        if r < len(SIZES) - 1:
            return
        for w in range(2):
            SX[n][w] = s_half(n, w, 1 - c).astype(BF)
        msgs["sx", n] = Message(SX[n], SC[n], dc=1)
        for w in range(2):
            SO[n % 2, w, :, : WIDTHS[n]] = s_half(n, w, c)

    update_scale = 0.2 * math.sqrt(max(M, N))

    def second_sum(r, n):
        if r < len(SIZES) - 1:
            return
        for w in range(2):
            for k in range(len(SIZES)):
                q = rows(xl * ROWS + xh * HALF + STARTS[k], SIZES[k])
                SO[n % 2, w, q, : WIDTHS[n]] = SO[n % 2, w, q, : WIDTHS[n]] + (coef_b / coef_c) * F[n][w, piece(k, y), :].astype(F32)
        msgs["sx", n].wait()
        for xx in range(4):
            q = pl.ds((xx % 2) * ROWS, ROWS)
            SP[n][xx] = (SO[n % 2, xx // 2, q, : WIDTHS[n]] + SC[n][xx // 2, q, :].astype(F32)).astype(BF)
        msgs["sv", n] = both(
            lambda d, w: Message(SP[n].at[mod4(x + 2), pl.ds(w * HALF, HALF)], SV[n].at[w], dx=d)
        )

    def second_near(r, n):
        if r < len(SIZES) - 1:
            return
        msgs["sr", n] = []
        for w, m in enumerate(msgs["sv", n]):
            m.wait()
            k = mod4(x + 1 - 2 * w)
            part = pl.ds(w * HALF, HALF)
            SP[n][k, part, :] = (SP[n][k, part, :].astype(F32) + SV[n][w].astype(F32)).astype(BF)
            msgs["sr", n].append(Message(SP[n].at[k], SR[n].at[w], dx=1 - 2 * w))

    def finish(r, n):
        if r < len(SIZES) - 1:
            return
        for m in msgs["sr", n]:
            m.wait()
        cols = slice(LEFT[n], LEFT[n] + WIDTHS[n])
        total = SP[n][x].astype(F32) + SR[n][0].astype(F32) + SR[n][1].astype(F32)
        rounded = x_ref[:, cols].astype(BF).astype(F32)
        o_ref[:, cols] = update_scale * (coef_a * rounded + coef_c * total)
        store = pltpu.make_async_copy(o_ref.at[:, cols], o_hbm.at[:, cols], io.at[1 + n])
        store.start()
        stores.append(store)

    stores = []
    def start(r, k):
        gram(r, k)
        z_far(r, k)

    start(0, 0)
    gather_end()
    start(0, 1)
    z_near(0, 0)
    start(1, 0)
    z_near(0, 1)
    z_sum(0, 0)
    start(1, 1)
    z_sum(0, 1)
    z_near(1, 0)
    z_pass(0, 0)
    z_near(1, 1)
    z_pass(0, 1)
    start(2, 0)
    start(2, 1)
    z_done(0)

    def pair(stage, r):
        return [(stage, (r, 0)), (stage, (r, 1))]

    steps = [(r, n) for r in range(len(SIZES)) for n in range(NC)]
    beside = {
        0: pair(z_sum, 1),
        1: pair(z_near, 2),
        2: pair(z_pass, 1) + [(transpose, (0,))],
        3: [(z_done, (1,))] + pair(z_sum, 2),
        5: pair(z_pass, 2) + [(transpose, (1,))],
        6: [(z_done, (2,))],
        7: [(transpose, (2,))],
    }
    stages = (f_first, f_near, f_sum, f_pass, second, second_sum, second_near, finish)
    for t in range(len(steps) + LAGS[-1]):
        for stage, lag in zip(stages, LAGS):
            if 0 <= t - lag < len(steps):
                stage(*steps[t - lag])
        for stage, which in beside.get(t, ()):
            stage(*which)

    for copy in sent:
        copy.wait_send()
    for store in stores:
        store.wait()


def body(iterate):
    hbm = pl.BlockSpec(memory_space=pltpu.HBM)

    def chunks(*extents):
        return [pltpu.VMEM(extents + (width,), BF) for width in WIDTHS]

    return pl.pallas_call(
        kernel,
        out_shape=jax.ShapeDtypeStruct((ROWS, COLS), F32),
        in_specs=[hbm],
        out_specs=hbm,
        scratch_shapes=[
            pltpu.VMEM((ROWS, COLS), F32),
            pltpu.VMEM((ROWS, COLS), F32),
            pltpu.VMEM((2, BLK, COLS), BF),
            pltpu.VMEM((4, 2, HALF, COLS), BF),
            pltpu.VMEM((SET, BLK), BF),
            pltpu.VMEM((2, Q, BLK), BF),
            pltpu.VMEM((2, HALF, BLK), BF),
            pltpu.VMEM((SET, BLK), BF),
            pltpu.VMEM((BLK, SET), BF),
            pltpu.VMEM((2, 2, SET, max(WIDTHS)), F32),
        ]
        + chunks(2, SET)
        + chunks(2, HALF)
        + chunks(2, 2, HALF)
        + chunks(2, SET)
        + chunks(2, SET)
        + chunks(2, SET)
        + chunks(4, ROWS)
        + chunks(2, HALF)
        + chunks(2, ROWS)
        + [
            pltpu.SemaphoreType.DMA((1 + NC,)),
            pltpu.SemaphoreType.DMA((256,)),
            pltpu.SemaphoreType.DMA((256,)),
        ],
        compiler_params=pltpu.CompilerParams(
            collective_id=0, has_side_effects=True, vmem_limit_bytes=62 * 2**20
        ),
        cost_estimate=pl.CostEstimate(flops=20_000_000_000, bytes_accessed=4_000_000, transcendentals=0),
    )(iterate)


def solution(mesh):
    grid = Mesh(mesh.devices.reshape(4, 2, 2, 4, 2), ("y", "xl", "core", "z", "xh"))
    spec = P(("y", "xl", "core"), ("z", "xh"))
    return jax.shard_map(body, mesh=grid, in_specs=(spec,), out_specs=spec, check_vma=False)
```

```python
import math

import jax
import jax.numpy as jnp
from jax import lax
from jax.experimental import pallas as pl
from jax.experimental.pallas import tpu as pltpu
from jax.sharding import Mesh
from jax.sharding import PartitionSpec as P

M = 7168
N = 8192

coef_a = 3.4445
coef_b = -4.775
coef_c = 2.0315

BF = jnp.bfloat16
F32 = jnp.float32
MESH = pl.DeviceIdType.MESH

ROWS = 448
COLS = 1024
HALF = 224
Q = 112
BLK = 1792
SET = 896
WIDTHS = (256, 256, 256, 256)
NC = len(WIDTHS)
LEFT = tuple(sum(WIDTHS[:n]) for n in range(NC))

SIZES = (64, 64, 96)
STARTS = tuple(sum(SIZES[:r]) for r in range(len(SIZES)))
ORDER = (
    ("g0",), ("g_ap",), ("g_far0",), ("g_bp0",), ("g_bpc0",), ("g_c2",), ("g_w1",), ("g_bp1",), ("start", 0, 0),
    ("z_near", 0, 0), ("g_far1",), ("g_end",), ("z_sum", 0, 0), ("g_end2",), ("start", 0, 1), ("g_bpc1",),
    ("z_near", 0, 1), ("z_pass", 0, 0), ("g_b",), ("z_sum", 0, 1), ("start", 1, 1), ("start", 1, 0),
    ("z_pass", 0, 1), ("z_near", 1, 1), ("start", 2, 0), ("z_done", 0), ("f_first", 0, 2), ("z_near", 1, 0),
    ("f_first", 0, 1), ("f_first", 0, 3), ("z_sum", 1, 1), ("f_first", 0, 0), ("f_near", 0, 2), ("f_near", 0, 1),
    ("z_sum", 1, 0), ("start", 2, 1), ("f_near", 0, 3), ("z_pass", 1, 1), ("f_sum", 0, 1), ("z_pass", 1, 0),
    ("f_near", 0, 0), ("f_sum", 0, 3), ("z_near", 2, 1), ("z_near", 2, 0), ("f_sum", 0, 2), ("z_done", 1),
    ("f_pass", 0, 1), ("f_first", 1, 3), ("transpose", 1), ("f_first", 1, 0), ("f_sum", 0, 0), ("f_first", 1, 2),
    ("f_near", 1, 3), ("z_sum", 2, 1), ("f_near", 1, 0), ("f_first", 1, 1), ("f_near", 1, 2), ("f_pass", 0, 2),
    ("f_pass", 0, 0), ("z_sum", 2, 0), ("f_sum", 1, 0), ("f_pass", 0, 3), ("z_pass", 2, 1), ("f_sum", 1, 2),
    ("f_pass", 1, 0), ("z_pass", 2, 0), ("f_near", 1, 1), ("f_sum", 1, 3), ("f_pass", 1, 2), ("z_done", 2),
    ("f_first", 2, 0), ("f_first", 2, 2), ("transpose", 0), ("f_near", 2, 0), ("f_first", 2, 3), ("f_sum", 2, 0),
    ("f_near", 2, 2), ("transpose", 2), ("f_pass", 2, 0), ("f_first", 2, 1), ("f_sum", 2, 2), ("f_near", 2, 3),
    ("second", 0), ("f_pass", 1, 3), ("second_own", 0), ("f_pass", 2, 2), ("f_near", 2, 1), ("second_sum", 0),
    ("f_sum", 2, 3), ("second", 2), ("f_sum", 2, 1), ("second_near", 0), ("second_own", 2), ("f_pass", 2, 3),
    ("second_sum", 2), ("f_sum", 1, 1), ("f_pass", 2, 1), ("second", 3), ("f_pass", 1, 1), ("second_own", 3),
    ("second_near", 2), ("second", 1), ("second_sum", 3), ("finish", 0), ("second_own", 1), ("second_sum", 1),
    ("second_near", 3), ("finish", 2), ("second_near", 1), ("finish", 3), ("finish", 1),
)

class Count:
    def __init__(self):
        self.n = 0

    def take(self):
        self.n += 1
        return self.n - 1


def mod4(v):
    return lax.rem(v + 8, 4)


def kernel(x_hbm, o_hbm, x_ref, o_ref, A, B, GP, GV, GR, G, GT, SO, *refs):
    FP, FV, FR, F, SX, SC, SP, SV, SR = [refs[k * NC : (k + 1) * NC] for k in range(9)]
    io, ss, rs = refs[9 * NC :]
    y = lax.axis_index("y")
    xl = lax.axis_index("xl")
    c = lax.axis_index("core")
    z = lax.axis_index("z")
    xh = lax.axis_index("xh")
    x = 2 * xh + xl
    count = Count()
    sent = []

    def at(dx=0, dy=0, dz=0, dc=0):
        xx = mod4(x + dx)
        return (mod4(y + dy), lax.rem(xx, 2), lax.rem(c + dc, 2), mod4(z + dz), lax.div(xx, 2))

    class Message:
        def __init__(self, src, dst, **to):
            k = count.take()
            self.copy = pltpu.make_async_remote_copy(
                src_ref=src, dst_ref=dst, send_sem=ss.at[k], recv_sem=rs.at[k], device_id=at(**to), device_id_type=MESH
            )
            sent.append(self.copy)
            self.copy.start()

        def wait(self):
            self.copy.wait_recv()

    def rows(start, size):
        return pl.ds(pl.multiple_of(start, 16), size)

    peers = [at(dx=k) for k in (1, 2, 3)] + [at(dy=k) for k in (1, 2, 3)] + [at(dz=k) for k in (1, 2, 3)]
    peers.append(at(dc=1))
    barrier = pltpu.get_barrier_semaphore()
    for peer in peers:
        pl.semaphore_signal(barrier, inc=1, device_id=peer, device_id_type=MESH)

    def a_slot(dx, off=0, size=ROWS):
        xx = mod4(x + dx)
        return A.at[lax.div(xx, 2), rows((2 * lax.rem(xx, 2) + c) * ROWS + off, size)]

    def near(dx):
        return lax.div(mod4(x + dx), 2) * HALF

    load = pltpu.make_async_copy(x_hbm, x_ref, io.at[0])
    load.start()
    load.wait()
    own = a_slot(0)
    own[...] = x_ref[...].astype(BF)
    B[y, xh] = x_ref[rows(near(0), HALF), :].astype(BF)
    pl.semaphore_wait(barrier, len(peers))

    def copy_slot(slot, off, size, **to):
        return Message(a_slot(slot, off, size), a_slot(slot, off, size), **to)

    def copy_b(step, w, off, size, **to):
        ref = B.at[mod4(y + step), w, pl.ds(off, size)]
        return Message(ref, ref, **to)

    def both(make):
        return [make(1 - 2 * w, w) for w in range(2)]

    msgs = {}
    PARTS = ((0, SIZES[0]), (SIZES[0], HALF - SIZES[0]))

    def gather_start():
        off, size = PARTS[0]
        msgs["b", 0] = both(lambda d, w: copy_b(0, xh, off, size, dy=d))
        msgs["far", 0] = copy_slot(0, near(2) + off, size, dx=2)
        msgs["an"] = both(lambda d, w: copy_slot(0, near(0), HALF, dx=d))
        msgs["af"] = both(lambda d, w: copy_slot(0, near(2), HALF, dx=d))
        off, size = PARTS[1]
        msgs["far", 1] = copy_slot(0, near(2) + off, size, dx=2)
        msgs["b", 1] = both(lambda d, w: copy_b(0, xh, off, size, dy=d))
        msgs["core", 0] = [copy_slot(0, 0, ROWS, dc=1)]

    def pass_b(kind, w_of, t):
        off, size = PARTS[t]
        msgs[kind + "p", t] = []
        for w, m in enumerate(msgs[kind, t]):
            m.wait()
            msgs[kind + "p", t].append(copy_b(2 * w - 1, w_of, off + w * (size // 2), size // 2, dy=1 - 2 * w))

    def gather_far(t):
        off, size = PARTS[t]
        msgs["far", t].wait()
        part = a_slot(2, near(0) + off, size)
        msgs["c", t] = both(lambda d, w: Message(part, B.at[y, 1 - xh, pl.ds(off, size)], dy=d))
        B[y, 1 - xh, pl.ds(off, size)] = part[...]
        if t:
            msgs["core", 3] = [copy_slot(2, near(0), HALF, dc=1)]

    def pass_a():
        msgs["ap"], msgs["core", 1] = [], []
        for w, m in enumerate(msgs["an"]):
            m.wait()
            msgs["ap"].append(copy_slot(2 * w - 1, near(2 * w - 1) + w * Q, Q, dx=1 - 2 * w))
            msgs["core", 1].append(copy_slot(2 * w - 1, near(2 * w - 1), HALF, dc=1))

    def gather_near():
        msgs["core", 2] = []
        for w, m in enumerate(msgs["af"]):
            m.wait()
            msgs["core", 2].append(copy_slot(2 * w - 1, near(2 * w + 1), HALF, dc=1))

    def wait_all(*kinds):
        for kind in kinds:
            for m in msgs[kind]:
                m.wait()

    def gather_far_end():
        wait_all("ap")
        msgs["core", 4] = [copy_slot(2, near(2), HALF, dc=1)]

    def piece(r, q, off=0, size=None):
        return rows(4 * STARTS[r] + mod4(q) * SIZES[r] + off, SIZES[r] if size is None else size)

    def cols_of(k):
        return pl.ds(pl.multiple_of((1 - xl if k == 0 else xl) * SET, 128), SET)

    def gram(r, k):
        cols = cols_of(k)
        acc = jnp.zeros((4 * SIZES[r], SET), F32)
        for w in range(2):
            left = B[:, w, STARTS[r] : STARTS[r] + SIZES[r], :].reshape(4 * SIZES[r], COLS)
            acc = acc + lax.dot_general(left, A[w, cols, :], (((1,), (1,)), ((), ())), preferred_element_type=F32)
        GP[pl.ds(4 * STARTS[r], 4 * SIZES[r]), cols] = acc.astype(BF)

    def z_far(r, k):
        h = SIZES[r] // 2
        msgs["zv", r, k] = both(
            lambda d, w: Message(
                GP.at[piece(r, z + 2, w * h, h), cols_of(k)], GV.at[w, pl.ds(STARTS[r] // 2, h), cols_of(k)], dz=d
            )
        )

    def z_near(r, k):
        h = SIZES[r] // 2
        msgs["zr", r, k] = []
        for w, m in enumerate(msgs["zv", r, k]):
            m.wait()
            q, cols = piece(r, z + 1 - 2 * w, w * h, h), cols_of(k)
            GP[q, cols] = (GP[q, cols].astype(F32) + GV[w, pl.ds(STARTS[r] // 2, h), cols].astype(F32)).astype(BF)
            msgs["zr", r, k].append(
                Message(
                    GP.at[piece(r, z + 1 - 2 * w), cols], GR.at[w, pl.ds(STARTS[r], SIZES[r]), cols], dz=1 - 2 * w
                )
            )

    def z_sum(r, k):
        for m in msgs["zr", r, k]:
            m.wait()
        part, cols = pl.ds(STARTS[r], SIZES[r]), cols_of(k)
        total = GP[piece(r, z), cols].astype(F32) + GR[0, part, cols].astype(F32) + GR[1, part, cols].astype(F32)
        G[piece(r, z), cols] = total.astype(BF)
        ref = G.at[piece(r, z), cols]
        msgs["zg", r, k] = both(lambda d, w: Message(ref, ref, dz=d))

    def z_pass(r, k):
        h = SIZES[r] // 2
        msgs["zp", r, k] = []
        for w, m in enumerate(msgs["zg", r, k]):
            m.wait()
            ref = G.at[piece(r, z - 1 + 2 * w, w * h, h), cols_of(k)]
            msgs["zp", r, k].append(Message(ref, ref, dz=1 - 2 * w))

    def z_done(r):
        for m in msgs["zp", r, 0] + msgs["zp", r, 1]:
            m.wait()

    def transpose(r):
        cols = slice(4 * STARTS[r], 4 * (STARTS[r] + SIZES[r]))
        for t in range(BLK // 256):
            GT[t * 256 : (t + 1) * 256, cols] = G[cols, t * 256 : (t + 1) * 256].T

    def beside(left, right, narrow):
        if not narrow:
            return [jnp.dot(left, right[w], preferred_element_type=F32) for w in range(2)]
        both_sides = jnp.dot(left, jnp.concatenate(right, axis=1), preferred_element_type=F32)
        return jnp.split(both_sides, 2, axis=1)

    def f_first(r, n):
        left = G[pl.ds(4 * STARTS[r], 4 * SIZES[r]), :]
        right = [A[w, :, LEFT[n] : LEFT[n] + WIDTHS[n]] for w in range(2)]
        for w, product in enumerate(beside(left, right, WIDTHS[n] < 256)):
            FP[n][w, pl.ds(4 * STARTS[r], 4 * SIZES[r]), :] = product.astype(BF)
        part = pl.ds(STARTS[r], SIZES[r])
        msgs["fv", r, n] = [
            Message(FP[n].at[w, piece(r, y + 2)], FV[n].at[w, part], dy=1 - 2 * w) for w in range(2)
        ]

    def f_near(r, n):
        part = pl.ds(STARTS[r], SIZES[r])
        msgs["fr", r, n] = []
        for w, m in enumerate(msgs["fv", r, n]):
            m.wait()
            q = piece(r, y + 1 - 2 * w)
            FP[n][w, q, :] = (FP[n][w, q, :].astype(F32) + FV[n][w, part, :].astype(F32)).astype(BF)
            msgs["fr", r, n].append(Message(FP[n].at[:, q], FR[n].at[w, :, part], dy=1 - 2 * w))

    def f_sum(r, n):
        part = pl.ds(STARTS[r], SIZES[r])
        for m in msgs["fr", r, n]:
            m.wait()
        q = piece(r, y)
        for w in range(2):
            total = FP[n][w, q, :].astype(F32) + FR[n][0, w, part, :].astype(F32) + FR[n][1, w, part, :].astype(F32)
            F[n][w, q, :] = total.astype(BF)
        msgs["fg", r, n] = [Message(F[n].at[:, q], F[n].at[:, q], dy=1 - 2 * w) for w in range(2)]

    def f_pass(r, n):
        msgs["fp", r, n] = []
        for w, m in enumerate(msgs["fg", r, n]):
            m.wait()
            ref = F[n].at[w, piece(r, y - 1 + 2 * w)]
            msgs["fp", r, n].append(Message(ref, ref, dy=1 - 2 * w))

    def s_half(n, core):
        left = [GT[rows(k * SET + core * ROWS, ROWS), :] for k in range(2)]
        return beside(jnp.concatenate(left, axis=0), [F[n][0], F[n][1]], WIDTHS[n] < 256)

    def second(n):
        for r in range(len(SIZES)):
            wait_all(("fp", r, n))
        for w, product in enumerate(s_half(n, 1 - c)):
            SX[n][w] = product.astype(BF)
        msgs["sx", n] = Message(SX[n], SC[n], dc=1)

    def second_own(n):
        for w, product in enumerate(s_half(n, c)):
            SO[n % 4, w, :, : WIDTHS[n]] = product

    update_scale = 0.2 * math.sqrt(max(M, N))

    def second_sum(n):
        for w in range(2):
            for k in range(len(SIZES)):
                q = rows(xl * ROWS + xh * HALF + STARTS[k], SIZES[k])
                SO[n % 4, w, q, : WIDTHS[n]] = SO[n % 4, w, q, : WIDTHS[n]] + (coef_b / coef_c) * F[n][w, piece(k, y), :].astype(F32)
        msgs["sx", n].wait()
        for xx in range(4):
            q = pl.ds((xx % 2) * ROWS, ROWS)
            SP[n][xx] = (SO[n % 4, xx // 2, q, : WIDTHS[n]] + SC[n][xx // 2, q, :].astype(F32)).astype(BF)
        msgs["sv", n] = both(
            lambda d, w: Message(SP[n].at[mod4(x + 2), pl.ds(w * HALF, HALF)], SV[n].at[w], dx=d)
        )

    def second_near(n):
        msgs["sr", n] = []
        for w, m in enumerate(msgs["sv", n]):
            m.wait()
            k = mod4(x + 1 - 2 * w)
            part = pl.ds(w * HALF, HALF)
            SP[n][k, part, :] = (SP[n][k, part, :].astype(F32) + SV[n][w].astype(F32)).astype(BF)
            msgs["sr", n].append(Message(SP[n].at[k], SR[n].at[w], dx=1 - 2 * w))

    def finish(n):
        for m in msgs["sr", n]:
            m.wait()
        cols = slice(LEFT[n], LEFT[n] + WIDTHS[n])
        total = SP[n][x].astype(F32) + SR[n][0].astype(F32) + SR[n][1].astype(F32)
        rounded = x_ref[:, cols].astype(BF).astype(F32)
        o_ref[:, cols] = update_scale * (coef_a * rounded + coef_c * total)
        store = pltpu.make_async_copy(o_ref.at[:, cols], o_hbm.at[:, cols], io.at[1 + n])
        store.start()
        stores.append(store)

    stores = []
    def start(r, k):
        gram(r, k)
        z_far(r, k)

    stages = {
        "g0": gather_start,
        "g_bp0": lambda: pass_b("b", xh, 0),
        "g_bp1": lambda: pass_b("b", xh, 1),
        "g_far0": lambda: gather_far(0),
        "g_far1": lambda: gather_far(1),
        "g_bpc0": lambda: pass_b("c", 1 - xh, 0),
        "g_bpc1": lambda: pass_b("c", 1 - xh, 1),
        "g_ap": pass_a,
        "g_c2": gather_near,
        "g_w1": lambda: wait_all(("bp", 0), ("cp", 0), ("core", 0), ("core", 1), ("core", 2)),
        "g_b": lambda: wait_all(("bp", 1), ("cp", 1)),
        "g_end": gather_far_end,
        "g_end2": lambda: wait_all(("core", 3), ("core", 4)),
        "start": start,
        "z_near": z_near,
        "z_sum": z_sum,
        "z_pass": z_pass,
        "z_done": z_done,
        "transpose": transpose,
        "f_first": f_first,
        "f_near": f_near,
        "f_sum": f_sum,
        "f_pass": f_pass,
        "second": second,
        "second_own": second_own,
        "second_sum": second_sum,
        "second_near": second_near,
        "finish": finish,
    }
    for stage, *which in ORDER:
        stages[stage](*which)

    for copy in sent:
        copy.wait_send()
    for store in stores:
        store.wait()


def body(iterate):
    hbm = pl.BlockSpec(memory_space=pltpu.HBM)

    def chunks(*extents):
        return [pltpu.VMEM(extents + (width,), BF) for width in WIDTHS]

    return pl.pallas_call(
        kernel,
        out_shape=jax.ShapeDtypeStruct((ROWS, COLS), F32),
        in_specs=[hbm],
        out_specs=hbm,
        scratch_shapes=[
            pltpu.VMEM((ROWS, COLS), F32),
            pltpu.VMEM((ROWS, COLS), F32),
            pltpu.VMEM((2, BLK, COLS), BF),
            pltpu.VMEM((4, 2, HALF, COLS), BF),
            pltpu.VMEM((SET, BLK), BF),
            pltpu.VMEM((2, Q, BLK), BF),
            pltpu.VMEM((2, HALF, BLK), BF),
            pltpu.VMEM((SET, BLK), BF),
            pltpu.VMEM((BLK, SET), BF),
            pltpu.VMEM((4, 2, SET, max(WIDTHS)), F32),
        ]
        + chunks(2, SET)
        + chunks(2, HALF)
        + chunks(2, 2, HALF)
        + chunks(2, SET)
        + chunks(2, SET)
        + chunks(2, SET)
        + chunks(4, ROWS)
        + chunks(2, HALF)
        + chunks(2, ROWS)
        + [
            pltpu.SemaphoreType.DMA((1 + NC,)),
            pltpu.SemaphoreType.DMA((256,)),
            pltpu.SemaphoreType.DMA((256,)),
        ],
        compiler_params=pltpu.CompilerParams(
            collective_id=0, has_side_effects=True, vmem_limit_bytes=62 * 2**20
        ),
        cost_estimate=pl.CostEstimate(flops=20_000_000_000, bytes_accessed=4_000_000, transcendentals=0),
    )(iterate)


def solution(mesh):
    grid = Mesh(mesh.devices.reshape(4, 2, 2, 4, 2), ("y", "xl", "core", "z", "xh"))
    spec = P(("y", "xl", "core"), ("z", "xh"))
    return jax.shard_map(body, mesh=grid, in_specs=(spec,), out_specs=spec, check_vma=False)
```

```python
import math

import jax
import jax.numpy as jnp
from jax import lax
from jax.experimental import pallas as pl
from jax.experimental.pallas import tpu as pltpu
from jax.sharding import Mesh
from jax.sharding import PartitionSpec as P

M = 7168
N = 8192

coef_a = 3.4445
coef_b = -4.775
coef_c = 2.0315

BF = jnp.bfloat16
F32 = jnp.float32
MESH = pl.DeviceIdType.MESH

ROWS = 448
COLS = 1024
HALF = 224
Q = 112
BLK = 1792
SET = 896
WIDTHS = (256, 256, 256, 256)
NC = len(WIDTHS)
LEFT = tuple(sum(WIDTHS[:n]) for n in range(NC))

SIZES = (64, 64, 96)
STARTS = tuple(sum(SIZES[:r]) for r in range(len(SIZES)))
(GATHER, B_NEAR_0, B_NEAR_1, FAR_0, FAR_1, B_FAR_0, B_FAR_1, A_PASS, A_NEAR, READY_0, READY_1,
    A_FAR, A_READY, START, Z_NEAR, Z_SUM, Z_PASS, Z_DONE, TRANSPOSE, F_FIRST, F_NEAR, F_SUM, F_PASS,
    SECOND, SECOND_OWN, SECOND_SUM, SECOND_NEAR, FINISH,) = range(28)
ORDER = (
    (GATHER,), (A_PASS,), (FAR_0,), (B_NEAR_0,), (B_FAR_0,), (A_NEAR,), (READY_0,), (B_NEAR_1,), (START, 0, 0),
    (Z_NEAR, 0, 0), (FAR_1,), (A_FAR,), (Z_SUM, 0, 0), (A_READY,), (START, 0, 1), (B_FAR_1,), (Z_NEAR, 0, 1),
    (Z_PASS, 0, 0), (READY_1,), (Z_SUM, 0, 1), (START, 1, 1), (START, 1, 0), (Z_PASS, 0, 1), (Z_NEAR, 1, 1),
    (START, 2, 0), (Z_DONE, 0), (F_FIRST, 0, 2), (Z_NEAR, 1, 0), (F_FIRST, 0, 1), (F_FIRST, 0, 3), (Z_SUM, 1, 1),
    (F_FIRST, 0, 0), (F_NEAR, 0, 2), (F_NEAR, 0, 1), (Z_SUM, 1, 0), (START, 2, 1), (F_NEAR, 0, 3), (Z_PASS, 1, 1),
    (F_SUM, 0, 1), (Z_PASS, 1, 0), (F_NEAR, 0, 0), (F_SUM, 0, 3), (Z_NEAR, 2, 1), (Z_NEAR, 2, 0), (F_SUM, 0, 2),
    (Z_DONE, 1), (F_PASS, 0, 1), (F_FIRST, 1, 3), (TRANSPOSE, 1), (F_FIRST, 1, 0), (F_SUM, 0, 0), (F_FIRST, 1, 2),
    (F_NEAR, 1, 3), (Z_SUM, 2, 1), (F_NEAR, 1, 0), (F_FIRST, 1, 1), (F_NEAR, 1, 2), (F_PASS, 0, 2), (F_PASS, 0, 0),
    (Z_SUM, 2, 0), (F_SUM, 1, 0), (F_PASS, 0, 3), (Z_PASS, 2, 1), (F_SUM, 1, 2), (F_PASS, 1, 0), (Z_PASS, 2, 0),
    (F_NEAR, 1, 1), (F_SUM, 1, 3), (F_PASS, 1, 2), (Z_DONE, 2), (F_FIRST, 2, 0), (F_FIRST, 2, 2), (TRANSPOSE, 0),
    (F_NEAR, 2, 0), (F_FIRST, 2, 3), (F_SUM, 2, 0), (F_NEAR, 2, 2), (TRANSPOSE, 2), (F_PASS, 2, 0), (F_FIRST, 2, 1),
    (F_SUM, 2, 2), (F_NEAR, 2, 3), (SECOND, 0), (F_PASS, 1, 3), (SECOND_OWN, 0), (F_PASS, 2, 2), (F_NEAR, 2, 1),
    (SECOND_SUM, 0), (F_SUM, 2, 3), (SECOND, 2), (F_SUM, 2, 1), (SECOND_NEAR, 0), (SECOND_OWN, 2), (F_PASS, 2, 3),
    (SECOND_SUM, 2), (F_SUM, 1, 1), (F_PASS, 2, 1), (SECOND, 3), (F_PASS, 1, 1), (SECOND_OWN, 3), (SECOND_NEAR, 2),
    (SECOND, 1), (SECOND_SUM, 3), (FINISH, 0), (SECOND_OWN, 1), (SECOND_SUM, 1), (SECOND_NEAR, 3), (FINISH, 2),
    (SECOND_NEAR, 1), (FINISH, 3), (FINISH, 1),
)


class Count:
    def __init__(self):
        self.n = 0

    def take(self):
        self.n += 1
        return self.n - 1


def mod4(v):
    return lax.rem(v + 8, 4)


def kernel(x_hbm, o_hbm, x_ref, o_ref, A, B, GP, GV, GR, G, GT, SO, *refs):
    FP, FV, FR, F, SX, SC, SP, SV, SR = [refs[k * NC : (k + 1) * NC] for k in range(9)]
    io, ss, rs = refs[9 * NC :]
    y = lax.axis_index("y")
    xl = lax.axis_index("xl")
    c = lax.axis_index("core")
    z = lax.axis_index("z")
    xh = lax.axis_index("xh")
    x = 2 * xh + xl
    count = Count()
    sent = []

    def at(dx=0, dy=0, dz=0, dc=0):
        xx = mod4(x + dx)
        return (mod4(y + dy), lax.rem(xx, 2), lax.rem(c + dc, 2), mod4(z + dz), lax.div(xx, 2))

    class Message:
        def __init__(self, src, dst, **to):
            k = count.take()
            self.copy = pltpu.make_async_remote_copy(
                src_ref=src, dst_ref=dst, send_sem=ss.at[k], recv_sem=rs.at[k], device_id=at(**to), device_id_type=MESH
            )
            sent.append(self.copy)
            self.copy.start()

        def wait(self):
            self.copy.wait_recv()

    def rows(start, size):
        return pl.ds(pl.multiple_of(start, 16), size)

    peers = [at(dx=k) for k in (1, 2, 3)] + [at(dy=k) for k in (1, 2, 3)] + [at(dz=k) for k in (1, 2, 3)]
    peers.append(at(dc=1))
    barrier = pltpu.get_barrier_semaphore()
    for peer in peers:
        pl.semaphore_signal(barrier, inc=1, device_id=peer, device_id_type=MESH)

    def a_slot(dx, off=0, size=ROWS):
        xx = mod4(x + dx)
        return A.at[lax.div(xx, 2), rows((2 * lax.rem(xx, 2) + c) * ROWS + off, size)]

    def near(dx):
        return lax.div(mod4(x + dx), 2) * HALF

    load = pltpu.make_async_copy(x_hbm, x_ref, io.at[0])
    load.start()
    load.wait()
    own = a_slot(0)
    own[...] = x_ref[...].astype(BF)
    B[y, xh] = x_ref[rows(near(0), HALF), :].astype(BF)
    pl.semaphore_wait(barrier, len(peers))

    def copy_slot(slot, off, size, **to):
        return Message(a_slot(slot, off, size), a_slot(slot, off, size), **to)

    def copy_b(step, w, off, size, **to):
        ref = B.at[mod4(y + step), w, pl.ds(off, size)]
        return Message(ref, ref, **to)

    def both(make):
        return [make(1 - 2 * w, w) for w in range(2)]

    msgs = {}
    PARTS = ((0, SIZES[0]), (SIZES[0], HALF - SIZES[0]))

    def gather_start():
        off, size = PARTS[0]
        msgs["b", 0] = both(lambda d, w: copy_b(0, xh, off, size, dy=d))
        msgs["far", 0] = copy_slot(0, near(2) + off, size, dx=2)
        msgs["an"] = both(lambda d, w: copy_slot(0, near(0), HALF, dx=d))
        msgs["af"] = both(lambda d, w: copy_slot(0, near(2), HALF, dx=d))
        off, size = PARTS[1]
        msgs["far", 1] = copy_slot(0, near(2) + off, size, dx=2)
        msgs["b", 1] = both(lambda d, w: copy_b(0, xh, off, size, dy=d))
        msgs["core", 0] = [copy_slot(0, 0, ROWS, dc=1)]

    def pass_b(kind, w_of, t):
        off, size = PARTS[t]
        msgs[kind + "p", t] = []
        for w, m in enumerate(msgs[kind, t]):
            m.wait()
            msgs[kind + "p", t].append(copy_b(2 * w - 1, w_of, off + w * (size // 2), size // 2, dy=1 - 2 * w))

    def gather_far(t):
        off, size = PARTS[t]
        msgs["far", t].wait()
        part = a_slot(2, near(0) + off, size)
        msgs["c", t] = both(lambda d, w: Message(part, B.at[y, 1 - xh, pl.ds(off, size)], dy=d))
        B[y, 1 - xh, pl.ds(off, size)] = part[...]
        if t:
            msgs["core", 3] = [copy_slot(2, near(0), HALF, dc=1)]

    def pass_a():
        msgs["ap"], msgs["core", 1] = [], []
        for w, m in enumerate(msgs["an"]):
            m.wait()
            msgs["ap"].append(copy_slot(2 * w - 1, near(2 * w - 1) + w * Q, Q, dx=1 - 2 * w))
            msgs["core", 1].append(copy_slot(2 * w - 1, near(2 * w - 1), HALF, dc=1))

    def gather_near():
        msgs["core", 2] = []
        for w, m in enumerate(msgs["af"]):
            m.wait()
            msgs["core", 2].append(copy_slot(2 * w - 1, near(2 * w + 1), HALF, dc=1))

    def wait_all(*kinds):
        for kind in kinds:
            for m in msgs[kind]:
                m.wait()

    def gather_far_end():
        wait_all("ap")
        msgs["core", 4] = [copy_slot(2, near(2), HALF, dc=1)]

    def piece(r, q, off=0, size=None):
        return rows(4 * STARTS[r] + mod4(q) * SIZES[r] + off, SIZES[r] if size is None else size)

    def cols_of(k):
        return pl.ds(pl.multiple_of((1 - xl if k == 0 else xl) * SET, 128), SET)

    def gram(r, k):
        cols = cols_of(k)
        acc = jnp.zeros((4 * SIZES[r], SET), F32)
        for w in range(2):
            left = B[:, w, STARTS[r] : STARTS[r] + SIZES[r], :].reshape(4 * SIZES[r], COLS)
            acc = acc + lax.dot_general(left, A[w, cols, :], (((1,), (1,)), ((), ())), preferred_element_type=F32)
        GP[pl.ds(4 * STARTS[r], 4 * SIZES[r]), cols] = acc.astype(BF)

    def z_far(r, k):
        h = SIZES[r] // 2
        msgs["zv", r, k] = both(
            lambda d, w: Message(
                GP.at[piece(r, z + 2, w * h, h), cols_of(k)], GV.at[w, pl.ds(STARTS[r] // 2, h), cols_of(k)], dz=d
            )
        )

    def z_near(r, k):
        h = SIZES[r] // 2
        msgs["zr", r, k] = []
        for w, m in enumerate(msgs["zv", r, k]):
            m.wait()
            q, cols = piece(r, z + 1 - 2 * w, w * h, h), cols_of(k)
            GP[q, cols] = (GP[q, cols].astype(F32) + GV[w, pl.ds(STARTS[r] // 2, h), cols].astype(F32)).astype(BF)
            msgs["zr", r, k].append(
                Message(
                    GP.at[piece(r, z + 1 - 2 * w), cols], GR.at[w, pl.ds(STARTS[r], SIZES[r]), cols], dz=1 - 2 * w
                )
            )

    def z_sum(r, k):
        for m in msgs["zr", r, k]:
            m.wait()
        part, cols = pl.ds(STARTS[r], SIZES[r]), cols_of(k)
        total = GP[piece(r, z), cols].astype(F32) + GR[0, part, cols].astype(F32) + GR[1, part, cols].astype(F32)
        G[piece(r, z), cols] = total.astype(BF)
        ref = G.at[piece(r, z), cols]
        msgs["zg", r, k] = both(lambda d, w: Message(ref, ref, dz=d))

    def z_pass(r, k):
        h = SIZES[r] // 2
        msgs["zp", r, k] = []
        for w, m in enumerate(msgs["zg", r, k]):
            m.wait()
            ref = G.at[piece(r, z - 1 + 2 * w, w * h, h), cols_of(k)]
            msgs["zp", r, k].append(Message(ref, ref, dz=1 - 2 * w))

    def z_done(r):
        for m in msgs["zp", r, 0] + msgs["zp", r, 1]:
            m.wait()

    def transpose(r):
        cols = slice(4 * STARTS[r], 4 * (STARTS[r] + SIZES[r]))
        for t in range(BLK // 256):
            GT[t * 256 : (t + 1) * 256, cols] = G[cols, t * 256 : (t + 1) * 256].T

    def beside(left, right, narrow):
        if not narrow:
            return [jnp.dot(left, right[w], preferred_element_type=F32) for w in range(2)]
        both_sides = jnp.dot(left, jnp.concatenate(right, axis=1), preferred_element_type=F32)
        return jnp.split(both_sides, 2, axis=1)

    def f_first(r, n):
        left = G[pl.ds(4 * STARTS[r], 4 * SIZES[r]), :]
        right = [A[w, :, LEFT[n] : LEFT[n] + WIDTHS[n]] for w in range(2)]
        for w, product in enumerate(beside(left, right, WIDTHS[n] < 256)):
            FP[n][w, pl.ds(4 * STARTS[r], 4 * SIZES[r]), :] = product.astype(BF)
        part = pl.ds(STARTS[r], SIZES[r])
        msgs["fv", r, n] = [
            Message(FP[n].at[w, piece(r, y + 2)], FV[n].at[w, part], dy=1 - 2 * w) for w in range(2)
        ]

    def f_near(r, n):
        part = pl.ds(STARTS[r], SIZES[r])
        msgs["fr", r, n] = []
        for w, m in enumerate(msgs["fv", r, n]):
            m.wait()
            q = piece(r, y + 1 - 2 * w)
            FP[n][w, q, :] = (FP[n][w, q, :].astype(F32) + FV[n][w, part, :].astype(F32)).astype(BF)
            msgs["fr", r, n].append(Message(FP[n].at[:, q], FR[n].at[w, :, part], dy=1 - 2 * w))

    def f_sum(r, n):
        part = pl.ds(STARTS[r], SIZES[r])
        for m in msgs["fr", r, n]:
            m.wait()
        q = piece(r, y)
        for w in range(2):
            total = FP[n][w, q, :].astype(F32) + FR[n][0, w, part, :].astype(F32) + FR[n][1, w, part, :].astype(F32)
            F[n][w, q, :] = total.astype(BF)
        msgs["fg", r, n] = [Message(F[n].at[:, q], F[n].at[:, q], dy=1 - 2 * w) for w in range(2)]

    def f_pass(r, n):
        msgs["fp", r, n] = []
        for w, m in enumerate(msgs["fg", r, n]):
            m.wait()
            ref = F[n].at[w, piece(r, y - 1 + 2 * w)]
            msgs["fp", r, n].append(Message(ref, ref, dy=1 - 2 * w))

    def s_half(n, core):
        left = [GT[rows(k * SET + core * ROWS, ROWS), :] for k in range(2)]
        return beside(jnp.concatenate(left, axis=0), [F[n][0], F[n][1]], WIDTHS[n] < 256)

    def second(n):
        for r in range(len(SIZES)):
            wait_all(("fp", r, n))
        for w, product in enumerate(s_half(n, 1 - c)):
            SX[n][w] = product.astype(BF)
        msgs["sx", n] = Message(SX[n], SC[n], dc=1)

    def second_own(n):
        for w, product in enumerate(s_half(n, c)):
            SO[n % 4, w, :, : WIDTHS[n]] = product

    update_scale = 0.2 * math.sqrt(max(M, N))

    def second_sum(n):
        for w in range(2):
            for k in range(len(SIZES)):
                q = rows(xl * ROWS + xh * HALF + STARTS[k], SIZES[k])
                SO[n % 4, w, q, : WIDTHS[n]] = SO[n % 4, w, q, : WIDTHS[n]] + (coef_b / coef_c) * F[n][w, piece(k, y), :].astype(F32)
        msgs["sx", n].wait()
        for xx in range(4):
            q = pl.ds((xx % 2) * ROWS, ROWS)
            SP[n][xx] = (SO[n % 4, xx // 2, q, : WIDTHS[n]] + SC[n][xx // 2, q, :].astype(F32)).astype(BF)
        msgs["sv", n] = both(
            lambda d, w: Message(SP[n].at[mod4(x + 2), pl.ds(w * HALF, HALF)], SV[n].at[w], dx=d)
        )

    def second_near(n):
        msgs["sr", n] = []
        for w, m in enumerate(msgs["sv", n]):
            m.wait()
            k = mod4(x + 1 - 2 * w)
            part = pl.ds(w * HALF, HALF)
            SP[n][k, part, :] = (SP[n][k, part, :].astype(F32) + SV[n][w].astype(F32)).astype(BF)
            msgs["sr", n].append(Message(SP[n].at[k], SR[n].at[w], dx=1 - 2 * w))

    def finish(n):
        for m in msgs["sr", n]:
            m.wait()
        cols = slice(LEFT[n], LEFT[n] + WIDTHS[n])
        total = SP[n][x].astype(F32) + SR[n][0].astype(F32) + SR[n][1].astype(F32)
        rounded = x_ref[:, cols].astype(BF).astype(F32)
        o_ref[:, cols] = update_scale * (coef_a * rounded + coef_c * total)
        store = pltpu.make_async_copy(o_ref.at[:, cols], o_hbm.at[:, cols], io.at[1 + n])
        store.start()
        stores.append(store)

    stores = []
    def start(r, k):
        gram(r, k)
        z_far(r, k)

    stages = {
        GATHER: gather_start,
        B_NEAR_0: lambda: pass_b("b", xh, 0),
        B_NEAR_1: lambda: pass_b("b", xh, 1),
        FAR_0: lambda: gather_far(0),
        FAR_1: lambda: gather_far(1),
        B_FAR_0: lambda: pass_b("c", 1 - xh, 0),
        B_FAR_1: lambda: pass_b("c", 1 - xh, 1),
        A_PASS: pass_a,
        A_NEAR: gather_near,
        READY_0: lambda: wait_all(("bp", 0), ("cp", 0), ("core", 0), ("core", 1), ("core", 2)),
        READY_1: lambda: wait_all(("bp", 1), ("cp", 1)),
        A_FAR: gather_far_end,
        A_READY: lambda: wait_all(("core", 3), ("core", 4)),
        START: start,
        Z_NEAR: z_near,
        Z_SUM: z_sum,
        Z_PASS: z_pass,
        Z_DONE: z_done,
        TRANSPOSE: transpose,
        F_FIRST: f_first,
        F_NEAR: f_near,
        F_SUM: f_sum,
        F_PASS: f_pass,
        SECOND: second,
        SECOND_OWN: second_own,
        SECOND_SUM: second_sum,
        SECOND_NEAR: second_near,
        FINISH: finish,
    }
    for stage, *which in ORDER:
        stages[stage](*which)

    for copy in sent:
        copy.wait_send()
    for store in stores:
        store.wait()


def body(iterate):
    hbm = pl.BlockSpec(memory_space=pltpu.HBM)

    def chunks(*extents):
        return [pltpu.VMEM(extents + (width,), BF) for width in WIDTHS]

    return pl.pallas_call(
        kernel,
        out_shape=jax.ShapeDtypeStruct((ROWS, COLS), F32),
        in_specs=[hbm],
        out_specs=hbm,
        scratch_shapes=[
            pltpu.VMEM((ROWS, COLS), F32),
            pltpu.VMEM((ROWS, COLS), F32),
            pltpu.VMEM((2, BLK, COLS), BF),
            pltpu.VMEM((4, 2, HALF, COLS), BF),
            pltpu.VMEM((SET, BLK), BF),
            pltpu.VMEM((2, Q, BLK), BF),
            pltpu.VMEM((2, HALF, BLK), BF),
            pltpu.VMEM((SET, BLK), BF),
            pltpu.VMEM((BLK, SET), BF),
            pltpu.VMEM((4, 2, SET, max(WIDTHS)), F32),
        ]
        + chunks(2, SET)
        + chunks(2, HALF)
        + chunks(2, 2, HALF)
        + chunks(2, SET)
        + chunks(2, SET)
        + chunks(2, SET)
        + chunks(4, ROWS)
        + chunks(2, HALF)
        + chunks(2, ROWS)
        + [
            pltpu.SemaphoreType.DMA((1 + NC,)),
            pltpu.SemaphoreType.DMA((256,)),
            pltpu.SemaphoreType.DMA((256,)),
        ],
        compiler_params=pltpu.CompilerParams(
            collective_id=0, has_side_effects=True, vmem_limit_bytes=62 * 2**20
        ),
        cost_estimate=pl.CostEstimate(flops=20_000_000_000, bytes_accessed=4_000_000, transcendentals=0),
    )(iterate)


def solution(mesh):
    grid = Mesh(mesh.devices.reshape(4, 2, 2, 4, 2), ("y", "xl", "core", "z", "xh"))
    spec = P(("y", "xl", "core"), ("z", "xh"))
    return jax.shard_map(body, mesh=grid, in_specs=(spec,), out_specs=spec, check_vma=False)
```
